32 devices in a mesh: row: 4 (over z), col: 8 (over y, x, core).
Axes of the slice: x: 2, y: 2, z: 4, core: 2. Of those that a mesh axis runs over, the one named last changes fastest.
Arguments:
- front: float32 [8192, 8192], P('row', 'col'), may hold values from -6 to 6
- inverses: float32 [2, 512, 512], replicated, may hold values from -2 to 2, as said below
- block_owner: int32 [64, 64], P('row', 'col'), may hold values from -1 to 31, as said below
- block_slot: int32 [64, 64], P('row', 'col'), may hold values from 0 to 47
- parent_in: float32 [1536, 128, 128], P(('row', 'col')), may hold values from -6 to 6
Outputs:
- updated: float32 [8192, 8192], P('row', 'col')
- panels: float32 [8192, 1024], P(('row', 'col'))
- parent_out: float32 [1536, 128, 128], P(('row', 'col'))
The draws below stay inside these ranges and needn't reach their ends.
Inputs may be any that keep to these rules, and one draw needn't show every extreme that they name: Entries of the pivot block inverses. `block_owner`: -1 exactly for blocks above the diagonal (I < J); on one device's 16 x 8 blocks no device is named more than 4 times, and on some device some device is named exactly 4 times.
All inputs are finite; a program needn't handle non-finite values.
Results may differ from the reference program's by a relative error of at most 0.00014.
Values sent between devices are 32-bit elements; how exact they have to be, the bound alone decides.
A program may use at most 128 MiB of HBM per device.

```python
import jax
import jax.numpy as jnp
from jax import lax

PW = 512
BS = 128
PSLOT = 48
F = 8192
NB = 64
TRB = 16
TCB = 8
NROWS = 4
NCOLS = 8
NDEV = 32
PB = 1536


def draw_inverses(key, part):
    key_diag, key_noise = jax.random.split(jax.random.fold_in(key, 11))
    diagonal = jax.random.uniform(key_diag, (2, PW), jnp.float32, 1.0, 2.0)
    noise = jax.random.normal(key_noise, (2, PW, PW), jnp.float32)
    symmetric = (noise + jnp.transpose(noise, (0, 2, 1))) * (0.6 / (PW * 1.4142135))
    identity = jnp.eye(PW, dtype=jnp.float32)
    return symmetric * (1.0 - identity) + identity * (diagonal[:, :, None] / jnp.sqrt(jnp.float32(PW)))


def draw_block_owner(key, part):
    candidates = jax.random.permutation(jax.random.fold_in(key, 5), NDEV).astype(jnp.int32)
    position = jnp.arange(NDEV, dtype=jnp.int32)
    sort_keys = jnp.where(candidates == 1, -2, jnp.where(candidates == NDEV // 2, -1, position)).astype(jnp.int32)
    offsets = candidates[jnp.argsort(sort_keys, stable=True)].astype(jnp.int32)
    index = jnp.arange(NB, dtype=jnp.int32)
    block_row = index[:, None] + jnp.zeros((NB, NB), jnp.int32)
    block_col = index[None, :] + jnp.zeros((NB, NB), jnp.int32)
    lower = (block_row >= block_col).astype(jnp.int32)
    tiles = lower.reshape(NROWS, TRB, NCOLS, TCB).transpose(0, 2, 1, 3).reshape(NROWS, NCOLS, TRB * TCB)
    ranks = jnp.cumsum(tiles, axis=2) - tiles
    ranks = ranks.reshape(NROWS, NCOLS, TRB, TCB).transpose(0, 2, 1, 3).reshape(NB, NB)
    source = block_row // TRB * NCOLS + block_col // TCB
    target = (source + offsets[ranks % NDEV]) % NDEV
    return jnp.where(lower > 0, target, -1).astype(jnp.int32)


def place_ends(entries, own_key, least, largest):
    longest = entries.shape.index(max(entries.shape))
    spots = []
    for shift in (0, 1):
        where = [jax.random.randint(jax.random.fold_in(own_key, axis), (), 0, length) for axis, length in enumerate(entries.shape)]
        where[longest] = (where[longest] + shift) % entries.shape[longest]
        spots.append(tuple(where))
    return entries.at[spots[0]].set(least).at[spots[1]].set(largest)


def block_levels(own_key, extent, cuts, low, largest):
    level = 1.0
    for dim, shards_of in cuts:
        heights = jax.random.uniform(jax.random.fold_in(jax.random.fold_in(own_key, 6), dim), (shards_of,), jnp.float32, low / len(cuts), largest / len(cuts))
        level = level * jnp.repeat(jnp.exp(heights), extent[dim] // shards_of).reshape((-1,) + (1,) * (len(extent) - 1 - dim))
    return level


def bell_draw(rng, dims, width, bound, shards=(), kind=jnp.bfloat16):
    entries = width * jax.random.normal(rng, dims, jnp.float32)
    if shards:
        entries = entries * block_levels(rng, dims, shards, -0.22, 0.18)
    return jnp.clip(entries, -bound, bound).astype(kind)


def setup_inputs(seed: int = 0) -> dict:
    keys = jax.random.split(jax.random.key(seed), 6)
    return {
        "front": bell_draw(keys[0], (F, F), 1.0, 6.0, ((0, 4), (1, 8)), jnp.float32),
        "inverses": draw_inverses(jax.random.fold_in(keys[5], 71), 0),
        "block_owner": draw_block_owner(jax.random.fold_in(keys[5], 71), 0),
        "block_slot": place_ends(jax.random.randint(keys[3], (NB, NB), 0, PSLOT), jax.random.fold_in(keys[3], 1), 0, PSLOT - 1).astype(jnp.int32),
        "parent_in": bell_draw(keys[4], (PB, BS, BS), 1.0, 6.0, ((0, 32),), jnp.float32),
    }


def matmul(left_side, right_side):
    return jnp.dot(left_side, right_side, preferred_element_type=jnp.float32, precision=lax.Precision.HIGHEST)


def reference(front, inverses, block_owner, block_slot, parent_in):
    factor_one = matmul(front[:, 0:PW], inverses[0])
    partial_value = front - matmul(factor_one, front[0:PW, :])
    factor_two = matmul(partial_value[:, PW:2 * PW], inverses[1])
    updated = partial_value - matmul(factor_two, partial_value[PW:2 * PW, :])
    panels = jnp.concatenate([factor_one, factor_two], axis=1)
    blocks = updated.reshape(NB, BS, NB, BS).transpose(0, 2, 1, 3).reshape(NB * NB, BS, BS)
    owners = block_owner.reshape(NB * NB)
    targets = jnp.where(owners >= 0, owners * PSLOT + block_slot.reshape(NB * NB), PB).astype(jnp.int32)
    added = jnp.zeros(parent_in.shape, parent_in.dtype).at[targets].add(blocks, mode="drop")
    parent_out = parent_in + added
    return updated, panels, parent_out
```

```python
import functools

import jax
import jax.numpy as jnp
from jax import lax
from jax.experimental import pallas as pl
from jax.experimental.pallas import tpu as pltpu
from jax.sharding import PartitionSpec as P

MESH = pl.DeviceIdType.MESH
ANY = pl.BlockSpec(memory_space=pl.ANY)
VMEM = pl.BlockSpec(memory_space=pltpu.VMEM)
SMEM = pl.BlockSpec(memory_space=pltpu.SMEM)


def matmul(left_side, right_side):
    return jnp.dot(
        left_side, right_side, preferred_element_type=jnp.float32, precision=lax.Precision.HIGH
    )


def chip_paths(chips):
    order = [i ^ (i >> 1) for i in range(chips)]
    if sorted(order) != list(range(chips)):
        order = list(range(chips))
    return order, [order[0]] + order[1:][::-1]


def pick(value, pairs, default):
    out = jnp.int32(default)
    for key, result in pairs:
        out = jnp.where(value == key, jnp.int32(result), out)
    return out


def spread_kernel(
    nrow, ncol, steps, cols_in, rows_in, cols_out, rows_out,
    row_send, row_recv, half_recv, chain_send, side_send, local_sem,
):
    row = lax.axis_index("row")
    col = lax.axis_index("col")
    chips = ncol // 2
    chip = col // 2
    core = col % 2
    paths = chip_paths(chips)
    half = cols_in.shape[0] // 2
    ch = half // steps
    rh = rows_in.shape[0] // steps
    nexts = [pick(chip, list(zip(p[:-1], p[1:])), 0) for p in paths]
    last = [p[-1] for p in paths]
    next_chip = jnp.where(core == 0, nexts[0], nexts[1])
    is_last = jnp.where(core == 0, chip == last[0], chip == last[1])

    def row_copy(src, k):
        s = pl.ds(k * rh, rh)
        return pltpu.make_async_remote_copy(
            src_ref=src.at[s, :], dst_ref=rows_out.at[s, :],
            send_sem=row_send.at[k], recv_sem=row_recv.at[k],
            device_id=(row + 1, col), device_id_type=MESH,
        )

    def col_copy(src, h, k, send, target):
        s = pl.ds(h * half + k * ch, ch)
        return pltpu.make_async_remote_copy(
            src_ref=src.at[s, :], dst_ref=cols_out.at[s, :],
            send_sem=send, recv_sem=half_recv.at[h, k],
            device_id=(row, target), device_id_type=MESH,
        )

    local_cols = pltpu.make_async_copy(cols_in, cols_out, local_sem.at[0])
    local_rows = pltpu.make_async_copy(rows_in, rows_out, local_sem.at[1])

    @pl.when(row == 0)
    def _():
        local_rows.start()

    @pl.when(col == 0)
    def _():
        local_cols.start()

    def step(k, carry):
        if nrow > 1:
            @pl.when(row == 0)
            def _():
                row_copy(rows_in, k).start()

            @pl.when(row > 0)
            def _():
                row_copy(rows_out, k).wait_recv()

            @pl.when((row > 0) & (row < nrow - 1))
            def _():
                row_copy(rows_out, k).start()

        @pl.when(col == 0)
        def _():
            if chips > 1:
                for h in range(2):
                    col_copy(cols_in, h, k, chain_send.at[h, k], paths[h][1] * 2 + h).start()
            for h in range(2):
                col_copy(cols_in, h, k, side_send.at[h, k], 1).start()

        @pl.when(chip > 0)
        def _():
            col_copy(cols_out, core, k, chain_send.at[core, k], 0).wait_recv()
            col_copy(cols_out, core, k, side_send.at[core, k], chip * 2 + 1 - core).start()

            @pl.when(jnp.logical_not(is_last))
            def _():
                col_copy(
                    cols_out, core, k, chain_send.at[core, k], next_chip * 2 + core
                ).start()

        return carry

    lax.fori_loop(0, steps, step, 0)

    def drain(k, carry):
        if nrow > 1:
            @pl.when(row < nrow - 1)
            def _():
                row_copy(rows_out, k).wait_send()

        @pl.when(col == 0)
        def _():
            for h in range(2):
                if chips > 1:
                    col_copy(cols_in, h, k, chain_send.at[h, k], 1).wait_send()
                col_copy(cols_in, h, k, side_send.at[h, k], 1).wait_send()

        @pl.when(col == 1)
        def _():
            for h in range(2):
                col_copy(cols_out, h, k, chain_send.at[h, k], 0).wait_recv()

        @pl.when(chip > 0)
        def _():
            col_copy(cols_out, 1 - core, k, chain_send.at[core, k], 0).wait_recv()
            col_copy(cols_out, core, k, side_send.at[core, k], 0).wait_send()

            @pl.when(jnp.logical_not(is_last))
            def _():
                col_copy(cols_out, core, k, chain_send.at[core, k], 0).wait_send()

        return carry

    lax.fori_loop(0, steps, drain, 0)

    @pl.when(row == 0)
    def _():
        local_rows.wait()

    @pl.when(col == 0)
    def _():
        local_cols.wait()


def spread(columns, rows, steps=32):
    nrow, ncol = lax.axis_size("row"), lax.axis_size("col")
    dma = pltpu.SemaphoreType.DMA
    return pl.pallas_call(
        functools.partial(spread_kernel, nrow, ncol, steps),
        out_shape=(
            jax.ShapeDtypeStruct(columns.shape, columns.dtype),
            jax.ShapeDtypeStruct(rows.shape, rows.dtype),
        ),
        in_specs=[ANY, ANY],
        out_specs=(VMEM, VMEM),
        scratch_shapes=[
            dma((steps,)), dma((steps,)), dma((2, steps)),
            dma((2, steps)), dma((2, steps)), dma((2,)),
        ],
        compiler_params=pltpu.CompilerParams(has_side_effects=True),
        name="spread",
    )(columns, rows)


def gather_kernel(count, bcols, where, updated, out, sem):
    edge = out.shape[1]

    def step(s, carry):
        b = where[s]
        src = updated.at[
            pl.ds(pl.multiple_of(b // bcols * edge, edge), edge),
            pl.ds(pl.multiple_of(b % bcols * edge, edge), edge),
        ]
        pltpu.make_async_copy(src, out.at[s], sem).start()
        return carry

    lax.fori_loop(0, count, step, 0)
    pltpu.make_async_copy(out, out, sem).wait()


def gather_blocks(where, updated, bcols, edge):
    count = where.shape[0]
    return pl.pallas_call(
        functools.partial(gather_kernel, count, bcols),
        out_shape=jax.ShapeDtypeStruct((count, edge, edge), updated.dtype),
        in_specs=[SMEM, ANY],
        out_specs=VMEM,
        scratch_shapes=[pltpu.SemaphoreType.DMA],
        name="gather_blocks",
    )(where, updated)


def exchange_kernel(
    nrow, ncol, brows, bcols, cap, blocks, labels, arrived, marks,
    send, recv, label_send, label_recv, local_sem,
):
    row = lax.axis_index("row")
    col = lax.axis_index("col")
    n = nrow * ncol
    me = row * ncol + col

    def active(r, c):
        return r * brows + brows - 1 >= c * bcols

    def block_copy(src, target):
        return pltpu.make_async_remote_copy(
            src_ref=blocks.at[pl.ds(target * cap, cap)], dst_ref=arrived.at[pl.ds(src * cap, cap)],
            send_sem=send.at[target], recv_sem=recv.at[src],
            device_id=(target // ncol, target % ncol), device_id_type=MESH,
        )

    def label_copy(src, target):
        return pltpu.make_async_remote_copy(
            src_ref=labels.at[target], dst_ref=marks.at[src],
            send_sem=label_send.at[target], recv_sem=label_recv.at[src],
            device_id=(target // ncol, target % ncol), device_id_type=MESH,
        )

    own_blocks = pltpu.make_async_copy(
        blocks.at[pl.ds(me * cap, cap)], arrived.at[pl.ds(me * cap, cap)], local_sem.at[0]
    )
    own_labels = pltpu.make_async_copy(labels.at[me], marks.at[me], local_sem.at[1])

    @pl.when(active(row, col))
    def _():
        def step(d, carry):
            target = (row + nrow - d % nrow) % nrow * ncol + (col + d // nrow) % ncol
            label_copy(me, target).start()
            block_copy(me, target).start()
            return carry

        lax.fori_loop(1, n, step, 0)
        own_blocks.start()
        own_labels.start()

    def arrive(s, carry):
        @pl.when((s != me) & active(s // ncol, s % ncol))
        def _():
            label_copy(s, 0).wait_recv()
            block_copy(s, 0).wait_recv()

        return carry

    lax.fori_loop(0, n, arrive, 0)

    @pl.when(active(row, col))
    def _():
        def drain(d, carry):
            target = (row + nrow - d % nrow) % nrow * ncol + (col + d // nrow) % ncol
            label_copy(me, target).wait_send()
            block_copy(me, target).wait_send()
            return carry

        lax.fori_loop(1, n, drain, 0)
        own_blocks.wait()
        own_labels.wait()


def exchange(blocks, labels, brows, bcols, cap):
    nrow, ncol = lax.axis_size("row"), lax.axis_size("col")
    n = nrow * ncol
    dma = pltpu.SemaphoreType.DMA
    return pl.pallas_call(
        functools.partial(exchange_kernel, nrow, ncol, brows, bcols, cap),
        out_shape=(
            jax.ShapeDtypeStruct(blocks.shape, blocks.dtype),
            jax.ShapeDtypeStruct(labels.shape, labels.dtype),
        ),
        in_specs=[VMEM, VMEM],
        out_specs=(VMEM, VMEM),
        scratch_shapes=[dma((n,)), dma((n,)), dma((n,)), dma((n,)), dma((2,))],
        compiler_params=pltpu.CompilerParams(has_side_effects=True),
        name="exchange",
    )(blocks, labels)


def add_kernel(per, marks, parent, arrived, out):
    g = pl.program_id(0)

    @pl.when(g == 0)
    def _():
        out[...] = parent[...]

    def step(i, carry):
        m = marks[g * per + i]

        @pl.when(m >= 0)
        def _():
            out[m] = out[m] + arrived[i]

        return carry

    lax.fori_loop(0, per, step, 0)


def add_blocks(marks, parent, arrived):
    count, edge, _ = arrived.shape
    per = count // 8 if count % 8 == 0 else count
    whole = pl.BlockSpec(parent.shape, lambda g: (0, 0, 0))
    return pl.pallas_call(
        functools.partial(add_kernel, per),
        grid=(count // per,),
        out_shape=jax.ShapeDtypeStruct(parent.shape, parent.dtype),
        in_specs=[SMEM, whole, pl.BlockSpec((per, edge, edge), lambda g: (g, 0, 0))],
        out_specs=whole,
        name="add_blocks",
    )(marks, parent, arrived)


def local(front, inverses, block_owner, block_slot, parent_in):
    width = inverses.shape[1]
    nrow, ncol = lax.axis_size("row"), lax.axis_size("col")
    devices = nrow * ncol
    row, col = lax.axis_index("row"), lax.axis_index("col")
    brows, bcols = block_owner.shape
    edge = parent_in.shape[1]
    count = brows * bcols
    cap = max(1, (count + devices - 1) // devices)

    owners = block_owner.reshape(1, count)
    slots = block_slot.reshape(1, 1, count)
    hit = owners == jnp.arange(devices, dtype=jnp.int32)[:, None]
    before = jnp.arange(count)[:, None] < jnp.arange(count)[None, :]
    rank = jnp.dot(
        hit.astype(jnp.float32), before.astype(jnp.float32), preferred_element_type=jnp.float32
    ).astype(jnp.int32)
    chosen = hit[:, None, :] & (rank[:, None, :] == jnp.arange(cap, dtype=jnp.int32)[:, None])
    position = jnp.arange(count, dtype=jnp.int32)
    where = jnp.sum(jnp.where(chosen, position, 0), axis=2).reshape(devices * cap)
    label = jnp.sum(jnp.where(chosen, slots + 1, 0), axis=2) - 1
    labels = jnp.broadcast_to(
        jnp.pad(label, ((0, 0), (0, 128 - cap)), constant_values=-1)[:, None, :], (devices, 8, 128)
    )

    factor_one, rows_one = spread(matmul(front[:, 0:width], inverses[0]), front[0:width, :])
    partial_value = front - matmul(factor_one, rows_one)
    factor_two, rows_two = spread(
        matmul(partial_value[:, width : 2 * width], inverses[1]),
        partial_value[width : 2 * width, :],
    )
    updated = partial_value - matmul(factor_two, rows_two)
    piece = front.shape[0] // ncol
    panels = jnp.concatenate(
        [
            lax.dynamic_slice_in_dim(factor_one, col * piece, piece, 0),
            lax.dynamic_slice_in_dim(factor_two, col * piece, piece, 0),
        ],
        axis=1,
    )

    blocks = gather_blocks(where, updated, bcols, edge)
    arrived, marks = exchange(blocks, labels, brows, bcols, cap)
    sources = jnp.arange(devices, dtype=jnp.int32)
    sends = sources // ncol * brows + brows - 1 >= sources % ncol * bcols
    marks = jnp.where(sends[:, None], marks[:, 0, :cap], -1).reshape(devices * cap)
    parent_out = add_blocks(marks, parent_in, arrived)
    return (updated, panels, parent_out)


def solution(mesh):
    in_specs = (
        P("row", "col"),
        P(),
        P("row", "col"),
        P("row", "col"),
        P(("row", "col"), None, None),
    )
    out_specs = (P("row", "col"), P(("row", "col"), None), P(("row", "col"), None, None))
    return jax.shard_map(local, mesh=mesh, in_specs=in_specs, out_specs=out_specs, check_vma=False)
```

```python
import functools

import jax
import jax.numpy as jnp
from jax import lax
from jax.experimental import pallas as pl
from jax.experimental.pallas import tpu as pltpu
from jax.sharding import PartitionSpec as P

MESH = pl.DeviceIdType.MESH
ANY = pl.BlockSpec(memory_space=pl.ANY)
VMEM = pl.BlockSpec(memory_space=pltpu.VMEM)
SMEM = pl.BlockSpec(memory_space=pltpu.SMEM)


def matmul(left_side, right_side):
    return jnp.dot(
        left_side, right_side, preferred_element_type=jnp.float32, precision=lax.Precision.HIGH
    )


def chip_paths(chips):
    order = [i ^ (i >> 1) for i in range(chips)]
    if sorted(order) != list(range(chips)):
        order = list(range(chips))
    return order, [order[0]] + order[1:][::-1]


def pick(value, pairs, default):
    out = jnp.int32(default)
    for key, result in pairs:
        out = jnp.where(value == key, jnp.int32(result), out)
    return out


def spread_kernel(
    nrow, ncol, width, front, cols_out, rows_out, corner_out,
    row_send, row_recv, half_recv, chain_send, side_send, local_sem,
):
    row = lax.axis_index("row")
    col = lax.axis_index("col")
    chips = ncol // 2
    chip = col // 2
    core = col % 2
    paths = chip_paths(chips)
    steps = 32
    half = cols_out.shape[0] // 2
    ch = half // steps
    quarter = steps // 2
    rh = width // quarter
    corner = steps // 4
    kh = width // 2 // corner
    nexts = [pick(chip, list(zip(p[:-1], p[1:])), 0) for p in paths]
    next_chip = jnp.where(core == 0, nexts[0], nexts[1])
    is_last = jnp.where(core == 0, chip == paths[0][-1], chip == paths[1][-1])
    pieces = ((1, 0), (0, 1), (0, 0), (1, 1))

    def row_copy(src, q, k):
        s = (pl.ds(pieces[q][0] * width + k * rh, rh), pl.ds(pieces[q][1] * width, width))
        return pltpu.make_async_remote_copy(
            src_ref=src.at[s], dst_ref=rows_out.at[s],
            send_sem=row_send.at[q * quarter + k], recv_sem=row_recv.at[q * quarter + k],
            device_id=(row + 1, col), device_id_type=MESH,
        )

    def col_copy(src, h, k, send, target):
        s = pl.ds(h * half + k * ch, ch)
        return pltpu.make_async_remote_copy(
            src_ref=src.at[s, :], dst_ref=cols_out.at[s, :],
            send_sem=send.at[h, k], recv_sem=half_recv.at[h, k],
            device_id=(row, target), device_id_type=MESH,
        )

    def corner_copy(src, first, h, k, i, send, target):
        at = h * (width // 2) + k * kh
        to = corner_out.at[i, pl.ds(at, kh), :]
        if first:
            src = src.at[pl.ds(pieces[i][0] * width + at, kh), pl.ds(pieces[i][1] * width, width)]
        else:
            src = to
        slot = steps + i * corner + k
        return pltpu.make_async_remote_copy(
            src_ref=src, dst_ref=to,
            send_sem=send.at[h, slot], recv_sem=half_recv.at[h, slot],
            device_id=(row, target), device_id_type=MESH,
        )

    local_cols = pltpu.make_async_copy(front, cols_out, local_sem.at[0])
    local_rows = pltpu.make_async_copy(
        front.at[pl.ds(0, 2 * width), :], rows_out, local_sem.at[1]
    )

    def local_corner(src, i):
        return pltpu.make_async_copy(
            src.at[pl.ds(pieces[i][0] * width, width), pl.ds(pieces[i][1] * width, width)],
            corner_out.at[i], local_sem.at[2 + i],
        )

    def source_sends(h, make):
        if chips > 1:
            make(h, chain_send, paths[h][1] * 2 + h).start()
        make(h, side_send, 1).start()

    @pl.when(row == 0)
    def _():
        if nrow > 1:
            for q in range(4):
                def first(k, carry, q=q):
                    row_copy(front, q, k).start()
                    return carry

                lax.fori_loop(0, quarter, first, 0)
        local_rows.start()

    @pl.when(col == 0)
    def _():
        def first(k, carry):
            for h in range(2):
                source_sends(h, lambda h, send, to: col_copy(front, h, k, send, to))
            return carry

        lax.fori_loop(0, steps, first, 0)
        local_cols.start()

    def pass_rows(q, k):
        if nrow > 1:
            @pl.when(row > 0)
            def _():
                row_copy(rows_out, q, k).wait_recv()

            @pl.when((row > 0) & (row < nrow - 1))
            def _():
                row_copy(rows_out, q, k).start()

    def pass_columns(make):
        @pl.when(chip > 0)
        def _():
            make(core, chain_send, 0).wait_recv()
            make(core, side_send, chip * 2 + 1 - core).start()

            @pl.when(jnp.logical_not(is_last))
            def _():
                make(core, chain_send, next_chip * 2 + core).start()

    for q in range(2):
        def both(k, carry, q=q):
            pass_rows(q, k)
            pass_columns(lambda h, send, to: col_copy(cols_out, h, q * quarter + k, send, to))
            return carry

        lax.fori_loop(0, quarter, both, 0)

    for i in range(2):
        @pl.when((col == 0) & (row == 0))
        def _(i=i):
            local_corner(front, i).start()

            def give(k, carry):
                for h in range(2):
                    source_sends(
                        h, lambda h, send, to: corner_copy(front, True, h, k, i, send, to)
                    )
                return carry

            lax.fori_loop(0, corner, give, 0)

        @pl.when((col == 0) & (row > 0))
        def _(i=i):
            local_corner(rows_out, i).start()

            def give(k, carry):
                for h in range(2):
                    source_sends(
                        h, lambda h, send, to: corner_copy(rows_out, True, h, k, i, send, to)
                    )
                return carry

            lax.fori_loop(0, corner, give, 0)

    for i in range(2):
        def third(k, carry, i=i):
            pass_rows(2, i * corner + k)
            pass_columns(
                lambda h, send, to: corner_copy(corner_out, False, h, k, i, send, to)
            )
            return carry

        lax.fori_loop(0, corner, third, 0)

    def fourth(k, carry):
        pass_rows(3, k)
        return carry

    lax.fori_loop(0, quarter, fourth, 0)

    if nrow > 1:
        @pl.when(row < nrow - 1)
        def _():
            for q in range(4):
                def sent(k, carry, q=q):
                    row_copy(rows_out, q, k).wait_send()
                    return carry

                lax.fori_loop(0, quarter, sent, 0)

    def drain(make):
        @pl.when(col == 0)
        def _():
            for h in range(2):
                if chips > 1:
                    make(h, chain_send).wait_send()
                make(h, side_send).wait_send()

        @pl.when(col == 1)
        def _():
            for h in range(2):
                make(h, chain_send).wait_recv()

        @pl.when(chip > 0)
        def _():
            make(1 - core, chain_send).wait_recv()
            make(core, side_send).wait_send()

            @pl.when(jnp.logical_not(is_last))
            def _():
                make(core, chain_send).wait_send()

    def drain_columns(k, carry):
        drain(lambda h, send: col_copy(cols_out, h, k, send, 0))
        return carry

    lax.fori_loop(0, steps, drain_columns, 0)
    for i in range(2):
        def drain_corner(k, carry, i=i):
            drain(lambda h, send: corner_copy(corner_out, False, h, k, i, send, 0))
            return carry

        lax.fori_loop(0, corner, drain_corner, 0)

    @pl.when(row == 0)
    def _():
        local_rows.wait()

    @pl.when(col == 0)
    def _():
        local_cols.wait()
        for i in range(2):
            local_corner(rows_out, i).wait()


def spread(front, width):
    nrow, ncol = lax.axis_size("row"), lax.axis_size("col")
    dma = pltpu.SemaphoreType.DMA
    shape = functools.partial(jax.ShapeDtypeStruct, dtype=front.dtype)
    return pl.pallas_call(
        functools.partial(spread_kernel, nrow, ncol, width),
        out_shape=(
            shape((front.shape[0], 2 * width)),
            shape((2 * width, front.shape[1])),
            shape((2, width, width)),
        ),
        in_specs=[ANY],
        out_specs=(VMEM, VMEM, VMEM),
        scratch_shapes=[
            dma((64,)), dma((64,)), dma((2, 48)), dma((2, 48)), dma((2, 48)), dma((4,)),
        ],
        compiler_params=pltpu.CompilerParams(has_side_effects=True),
        name="spread",
    )(front)


def gather_kernel(count, bcols, where, updated, out, sem):
    edge = out.shape[1]

    def step(s, carry):
        b = where[s]
        src = updated.at[
            pl.ds(pl.multiple_of(b // bcols * edge, edge), edge),
            pl.ds(pl.multiple_of(b % bcols * edge, edge), edge),
        ]
        pltpu.make_async_copy(src, out.at[s], sem).start()
        return carry

    lax.fori_loop(0, count, step, 0)
    pltpu.make_async_copy(out, out, sem).wait()


def gather_blocks(where, updated, bcols, edge):
    count = where.shape[0]
    return pl.pallas_call(
        functools.partial(gather_kernel, count, bcols),
        out_shape=jax.ShapeDtypeStruct((count, edge, edge), updated.dtype),
        in_specs=[SMEM, ANY],
        out_specs=VMEM,
        scratch_shapes=[pltpu.SemaphoreType.DMA],
        name="gather_blocks",
    )(where, updated)


def exchange_kernel(
    nrow, ncol, brows, bcols, cap, blocks, labels, arrived, marks, middle,
    send, middle_recv, pass_send, recv, label_send, label_recv, local_sem,
):
    row = lax.axis_index("row")
    col = lax.axis_index("col")
    n = nrow * ncol
    me = row * ncol + col

    def active(r, c):
        return r * brows + brows - 1 >= c * bcols

    def piece(index):
        return pl.ds(index * cap, cap)

    def hop(to_row, to_col):
        target = to_row * ncol + to_col
        return pltpu.make_async_remote_copy(
            src_ref=blocks.at[piece(target)], dst_ref=middle.at[piece(to_row * ncol + col)],
            send_sem=send.at[target], recv_sem=middle_recv.at[to_row * ncol + col],
            device_id=(row, to_col), device_id_type=MESH,
        )

    def relay(to_row, from_col):
        return pltpu.make_async_remote_copy(
            src_ref=middle.at[piece(to_row * ncol + from_col)],
            dst_ref=arrived.at[piece(row * ncol + from_col)],
            send_sem=pass_send.at[to_row * ncol + from_col],
            recv_sem=recv.at[row * ncol + from_col],
            device_id=(to_row, col), device_id_type=MESH,
        )

    def straight(source, target):
        return pltpu.make_async_remote_copy(
            src_ref=blocks.at[piece(target)], dst_ref=arrived.at[piece(source)],
            send_sem=send.at[target], recv_sem=recv.at[source],
            device_id=(target // ncol, target % ncol), device_id_type=MESH,
        )

    def label_copy(source, target):
        return pltpu.make_async_remote_copy(
            src_ref=labels.at[target], dst_ref=marks.at[source],
            send_sem=label_send.at[target], recv_sem=label_recv.at[source],
            device_id=(target // ncol, target % ncol), device_id_type=MESH,
        )

    own_blocks = pltpu.make_async_copy(blocks.at[piece(me)], arrived.at[piece(me)], local_sem.at[0])
    own_labels = pltpu.make_async_copy(labels.at[me], marks.at[me], local_sem.at[1])

    order = [(nrow // 2 + i) % nrow for i in range(nrow)]
    order = [o for o in order if o != 0]

    @pl.when(active(row, col))
    def _():
        for o in order:
            straight(me, (row + o) % nrow * ncol + col).start()

        def step(j, carry):
            to_col = (col + j) % ncol
            for o in order:
                hop((row + o) % nrow, to_col).start()
            return carry

        lax.fori_loop(1, ncol, step, 0)

        def inside(j, carry):
            straight(me, row * ncol + (col + j) % ncol).start()
            return carry

        lax.fori_loop(1, ncol, inside, 0)

        def label_step(d, carry):
            label_copy(me, (me + d) % n).start()
            return carry

        lax.fori_loop(1, n, label_step, 0)
        own_blocks.start()
        own_labels.start()

    def forward(j, carry):
        from_col = (col + ncol - j) % ncol

        @pl.when(active(row, from_col))
        def _():
            for o in order:
                to_row = (row + o) % nrow
                pltpu.make_async_remote_copy(
                    src_ref=blocks.at[piece(0)],
                    dst_ref=middle.at[piece(to_row * ncol + from_col)],
                    send_sem=send.at[0], recv_sem=middle_recv.at[to_row * ncol + from_col],
                    device_id=(row, from_col), device_id_type=MESH,
                ).wait_recv()
                relay(to_row, from_col).start()

        return carry

    lax.fori_loop(1, ncol, forward, 0)

    def arrive(s, carry):
        @pl.when((s != me) & active(s // ncol, s % ncol))
        def _():
            label_copy(s, 0).wait_recv()
            straight(s, 0).wait_recv()

        return carry

    lax.fori_loop(0, n, arrive, 0)

    def passed(j, carry):
        from_col = (col + ncol - j) % ncol

        @pl.when(active(row, from_col))
        def _():
            for o in order:
                relay((row + o) % nrow, from_col).wait_send()

        return carry

    lax.fori_loop(1, ncol, passed, 0)

    @pl.when(active(row, col))
    def _():
        def drain(d, carry):
            target = (me + d) % n
            label_copy(me, target).wait_send()
            straight(me, target).wait_send()
            return carry

        lax.fori_loop(1, n, drain, 0)
        own_blocks.wait()
        own_labels.wait()


def exchange(blocks, labels, brows, bcols, cap):
    nrow, ncol = lax.axis_size("row"), lax.axis_size("col")
    n = nrow * ncol
    dma = pltpu.SemaphoreType.DMA
    return pl.pallas_call(
        functools.partial(exchange_kernel, nrow, ncol, brows, bcols, cap),
        out_shape=(
            jax.ShapeDtypeStruct(blocks.shape, blocks.dtype),
            jax.ShapeDtypeStruct(labels.shape, labels.dtype),
        ),
        in_specs=[VMEM, VMEM],
        out_specs=(VMEM, VMEM),
        scratch_shapes=[
            pltpu.VMEM(blocks.shape, blocks.dtype),
            dma((n,)), dma((n,)), dma((n,)), dma((n,)), dma((n,)), dma((n,)), dma((2,)),
        ],
        compiler_params=pltpu.CompilerParams(has_side_effects=True),
        name="exchange",
    )(blocks, labels)


def add_kernel(per, marks, parent, arrived, out):
    g = pl.program_id(0)

    @pl.when(g == 0)
    def _():
        out[...] = parent[...]

    def step(i, carry):
        m = marks[g * per + i]

        @pl.when(m >= 0)
        def _():
            out[m] = out[m] + arrived[i]

        return carry

    lax.fori_loop(0, per, step, 0)


def add_blocks(marks, parent, arrived):
    count, edge, _ = arrived.shape
    per = count // 8 if count % 8 == 0 else count
    whole = pl.BlockSpec(parent.shape, lambda g: (0, 0, 0))
    return pl.pallas_call(
        functools.partial(add_kernel, per),
        grid=(count // per,),
        out_shape=jax.ShapeDtypeStruct(parent.shape, parent.dtype),
        in_specs=[SMEM, whole, pl.BlockSpec((per, edge, edge), lambda g: (g, 0, 0))],
        out_specs=whole,
        name="add_blocks",
    )(marks, parent, arrived)


def local(front, inverses, block_owner, block_slot, parent_in):
    width = inverses.shape[1]
    nrow, ncol = lax.axis_size("row"), lax.axis_size("col")
    devices = nrow * ncol
    row, col = lax.axis_index("row"), lax.axis_index("col")
    brows, bcols = block_owner.shape
    edge = parent_in.shape[1]
    count = brows * bcols
    cap = max(1, (count + devices - 1) // devices)

    owners = block_owner.reshape(1, count)
    slots = block_slot.reshape(1, 1, count)
    hit = owners == jnp.arange(devices, dtype=jnp.int32)[:, None]
    before = jnp.arange(count)[:, None] < jnp.arange(count)[None, :]
    rank = jnp.dot(
        hit.astype(jnp.float32), before.astype(jnp.float32), preferred_element_type=jnp.float32
    ).astype(jnp.int32)
    chosen = hit[:, None, :] & (rank[:, None, :] == jnp.arange(cap, dtype=jnp.int32)[:, None])
    position = jnp.arange(count, dtype=jnp.int32)
    where = jnp.sum(jnp.where(chosen, position, 0), axis=2).reshape(devices * cap)
    label = jnp.sum(jnp.where(chosen, slots + 1, 0), axis=2) - 1
    labels = jnp.broadcast_to(
        jnp.pad(label, ((0, 0), (0, 128 - cap)), constant_values=-1)[:, None, :], (devices, 8, 128)
    )

    columns, rows, corner = spread(front, width)
    below, right = corner[0], corner[1]
    rows_one = rows[:width]
    factor_one = matmul(columns[:, :width], inverses[0])
    factor_two = matmul(columns[:, width:] - matmul(factor_one, right), inverses[1])
    rows_two = rows[width:] - matmul(matmul(below, inverses[0]), rows_one)
    updated = front - matmul(factor_one, rows_one) - matmul(factor_two, rows_two)
    piece = front.shape[0] // ncol
    panels = jnp.concatenate(
        [
            lax.dynamic_slice_in_dim(factor_one, col * piece, piece, 0),
            lax.dynamic_slice_in_dim(factor_two, col * piece, piece, 0),
        ],
        axis=1,
    )

    blocks = gather_blocks(where, updated, bcols, edge)
    arrived, marks = exchange(blocks, labels, brows, bcols, cap)
    sources = jnp.arange(devices, dtype=jnp.int32)
    sends = sources // ncol * brows + brows - 1 >= sources % ncol * bcols
    marks = jnp.where(sends[:, None], marks[:, 0, :cap], -1).reshape(devices * cap)
    parent_out = add_blocks(marks, parent_in, arrived)
    return (updated, panels, parent_out)


def solution(mesh):
    in_specs = (
        P("row", "col"),
        P(),
        P("row", "col"),
        P("row", "col"),
        P(("row", "col"), None, None),
    )
    out_specs = (P("row", "col"), P(("row", "col"), None), P(("row", "col"), None, None))
    return jax.shard_map(local, mesh=mesh, in_specs=in_specs, out_specs=out_specs, check_vma=False)
```

```python
import functools

import jax
import jax.numpy as jnp
from jax import lax
from jax.experimental import pallas as pl
from jax.experimental.pallas import tpu as pltpu
from jax.sharding import PartitionSpec as P

MESH = pl.DeviceIdType.MESH
ANY = pl.BlockSpec(memory_space=pl.ANY)
VMEM = pl.BlockSpec(memory_space=pltpu.VMEM)
SMEM = pl.BlockSpec(memory_space=pltpu.SMEM)


def matmul(left_side, right_side):
    return jnp.dot(
        left_side, right_side, preferred_element_type=jnp.float32, precision=lax.Precision.HIGH
    )


def chip_paths(chips):
    order = [i ^ (i >> 1) for i in range(chips)]
    if sorted(order) != list(range(chips)):
        order = list(range(chips))
    return order, [order[0]] + order[1:][::-1]


def pick(value, pairs, default):
    out = jnp.int32(default)
    for key, result in pairs:
        out = jnp.where(value == key, jnp.int32(result), out)
    return out


def spread_kernel(
    nrow, ncol, width, front, cols_out, rows_out, corner_out,
    stage_cols, stage_rows, stage_corner,
    row_send, row_recv, half_recv, chain_send, side_send, local_sem,
):
    row = lax.axis_index("row")
    col = lax.axis_index("col")
    chips = ncol // 2
    chip = col // 2
    core = col % 2
    paths = chip_paths(chips)
    steps = 32
    half = cols_out.shape[0] // 2
    ch = half // steps
    quarter = steps // 2
    rh = width // quarter
    corner = steps // 4
    kh = width // 2 // corner
    nexts = [pick(chip, list(zip(p[:-1], p[1:])), 0) for p in paths]
    next_chip = jnp.where(core == 0, nexts[0], nexts[1])
    is_last = jnp.where(core == 0, chip == paths[0][-1], chip == paths[1][-1])
    pieces = ((1, 0), (0, 1), (0, 0), (1, 1))

    def row_copy(src, q, k):
        s = (pl.ds(pieces[q][0] * width + k * rh, rh), pl.ds(pieces[q][1] * width, width))
        return pltpu.make_async_remote_copy(
            src_ref=src.at[s], dst_ref=rows_out.at[s],
            send_sem=row_send.at[q * quarter + k], recv_sem=row_recv.at[q * quarter + k],
            device_id=(row + 1, col), device_id_type=MESH,
        )

    def col_copy(src, h, k, send, target):
        s = pl.ds(h * half + k * ch, ch)
        return pltpu.make_async_remote_copy(
            src_ref=src.at[s, :], dst_ref=cols_out.at[s, :],
            send_sem=send.at[h, k], recv_sem=half_recv.at[h, k],
            device_id=(row, target), device_id_type=MESH,
        )

    def corner_copy(src, first, h, k, i, send, target):
        at = h * (width // 2) + k * kh
        to = corner_out.at[i, pl.ds(at, kh), :]
        if first:
            src = src.at[pl.ds(pieces[i][0] * width + at, kh), pl.ds(pieces[i][1] * width, width)]
        else:
            src = to
        slot = steps + i * corner + k
        return pltpu.make_async_remote_copy(
            src_ref=src, dst_ref=to,
            send_sem=send.at[h, slot], recv_sem=half_recv.at[h, slot],
            device_id=(row, target), device_id_type=MESH,
        )

    local_cols = pltpu.make_async_copy(front, stage_cols, local_sem.at[0])
    local_rows = pltpu.make_async_copy(
        front.at[pl.ds(0, 2 * width), :], stage_rows, local_sem.at[1]
    )

    def local_corner(src, i):
        return pltpu.make_async_copy(
            src.at[pl.ds(pieces[i][0] * width, width), pl.ds(pieces[i][1] * width, width)],
            stage_corner.at[i], local_sem.at[2 + i],
        )

    def store(stage, out, i):
        return pltpu.make_async_copy(stage, out, local_sem.at[4 + i])

    def source_sends(h, make):
        if chips > 1:
            make(h, chain_send, paths[h][1] * 2 + h).start()
        make(h, side_send, 1).start()

    @pl.when(row == 0)
    def _():
        if nrow > 1:
            for q in range(4):
                def first(k, carry, q=q):
                    row_copy(front, q, k).start()
                    return carry

                lax.fori_loop(0, quarter, first, 0)
        local_rows.start()

    @pl.when(col == 0)
    def _():
        def first(k, carry):
            for h in range(2):
                source_sends(h, lambda h, send, to: col_copy(front, h, k, send, to))
            return carry

        lax.fori_loop(0, steps, first, 0)
        local_cols.start()

    def pass_rows(q, k):
        if nrow > 1:
            @pl.when(row > 0)
            def _():
                row_copy(rows_out, q, k).wait_recv()

            @pl.when((row > 0) & (row < nrow - 1))
            def _():
                row_copy(rows_out, q, k).start()

    def pass_columns(make):
        @pl.when(chip > 0)
        def _():
            make(core, chain_send, 0).wait_recv()
            make(core, side_send, chip * 2 + 1 - core).start()

            @pl.when(jnp.logical_not(is_last))
            def _():
                make(core, chain_send, next_chip * 2 + core).start()

    for q in range(2):
        def both(k, carry, q=q):
            pass_rows(q, k)
            pass_columns(lambda h, send, to: col_copy(cols_out, h, q * quarter + k, send, to))
            return carry

        lax.fori_loop(0, quarter, both, 0)

    for i in range(2):
        @pl.when((col == 0) & (row == 0))
        def _(i=i):
            local_corner(front, i).start()

            def give(k, carry):
                for h in range(2):
                    source_sends(
                        h, lambda h, send, to: corner_copy(front, True, h, k, i, send, to)
                    )
                return carry

            lax.fori_loop(0, corner, give, 0)

        @pl.when((col == 0) & (row > 0))
        def _(i=i):
            local_corner(rows_out, i).start()

            def give(k, carry):
                for h in range(2):
                    source_sends(
                        h, lambda h, send, to: corner_copy(rows_out, True, h, k, i, send, to)
                    )
                return carry

            lax.fori_loop(0, corner, give, 0)

    for i in range(2):
        def third(k, carry, i=i):
            pass_rows(2, i * corner + k)
            pass_columns(
                lambda h, send, to: corner_copy(corner_out, False, h, k, i, send, to)
            )
            return carry

        lax.fori_loop(0, corner, third, 0)

    @pl.when(row == 0)
    def _():
        local_rows.wait()
        store(stage_rows, rows_out, 1).start()

    @pl.when(col == 0)
    def _():
        local_cols.wait()
        store(stage_cols, cols_out, 0).start()
        for i in range(2):
            local_corner(rows_out, i).wait()
        store(stage_corner, corner_out, 2).start()

    def fourth(k, carry):
        pass_rows(3, k)
        return carry

    lax.fori_loop(0, quarter, fourth, 0)

    if nrow > 1:
        @pl.when(row < nrow - 1)
        def _():
            for q in range(4):
                def sent(k, carry, q=q):
                    row_copy(rows_out, q, k).wait_send()
                    return carry

                lax.fori_loop(0, quarter, sent, 0)

    def drain(make):
        @pl.when(col == 0)
        def _():
            for h in range(2):
                if chips > 1:
                    make(h, chain_send).wait_send()
                make(h, side_send).wait_send()

        @pl.when(col == 1)
        def _():
            for h in range(2):
                make(h, chain_send).wait_recv()

        @pl.when(chip > 0)
        def _():
            make(1 - core, chain_send).wait_recv()
            make(core, side_send).wait_send()

            @pl.when(jnp.logical_not(is_last))
            def _():
                make(core, chain_send).wait_send()

    def drain_columns(k, carry):
        drain(lambda h, send: col_copy(cols_out, h, k, send, 0))
        return carry

    lax.fori_loop(0, steps, drain_columns, 0)
    for i in range(2):
        def drain_corner(k, carry, i=i):
            drain(lambda h, send: corner_copy(corner_out, False, h, k, i, send, 0))
            return carry

        lax.fori_loop(0, corner, drain_corner, 0)

    @pl.when(row == 0)
    def _():
        store(stage_rows, rows_out, 1).wait()

    @pl.when(col == 0)
    def _():
        store(stage_cols, cols_out, 0).wait()
        store(stage_corner, corner_out, 2).wait()


def spread(front, width):
    nrow, ncol = lax.axis_size("row"), lax.axis_size("col")
    dma = pltpu.SemaphoreType.DMA
    shape = functools.partial(jax.ShapeDtypeStruct, dtype=front.dtype)
    return pl.pallas_call(
        functools.partial(spread_kernel, nrow, ncol, width),
        out_shape=(
            shape((front.shape[0], 2 * width)),
            shape((2 * width, front.shape[1])),
            shape((2, width, width)),
        ),
        in_specs=[ANY],
        out_specs=(ANY, ANY, ANY),
        scratch_shapes=[
            pltpu.VMEM((front.shape[0], 2 * width), front.dtype),
            pltpu.VMEM((2 * width, front.shape[1]), front.dtype),
            pltpu.VMEM((2, width, width), front.dtype),
            dma((64,)), dma((64,)), dma((2, 48)), dma((2, 48)), dma((2, 48)), dma((7,)),
        ],
        compiler_params=pltpu.CompilerParams(has_side_effects=True),
        name="spread",
    )(front)


def gather_kernel(count, bcols, where, updated, out, sem):
    edge = out.shape[1]

    def step(s, carry):
        b = where[s]
        src = updated.at[
            pl.ds(pl.multiple_of(b // bcols * edge, edge), edge),
            pl.ds(pl.multiple_of(b % bcols * edge, edge), edge),
        ]
        pltpu.make_async_copy(src, out.at[s], sem).start()
        return carry

    lax.fori_loop(0, count, step, 0)
    pltpu.make_async_copy(out, out, sem).wait()


def gather_blocks(where, updated, bcols, edge):
    count = where.shape[0]
    return pl.pallas_call(
        functools.partial(gather_kernel, count, bcols),
        out_shape=jax.ShapeDtypeStruct((count, edge, edge), updated.dtype),
        in_specs=[SMEM, ANY],
        out_specs=VMEM,
        scratch_shapes=[pltpu.SemaphoreType.DMA],
        name="gather_blocks",
    )(where, updated)


def exchange_kernel(
    nrow, ncol, brows, bcols, cap, blocks, labels, arrived, marks, middle,
    send, middle_recv, pass_send, recv, label_send, label_recv, local_sem,
):
    row = lax.axis_index("row")
    col = lax.axis_index("col")
    n = nrow * ncol
    me = row * ncol + col

    def active(r, c):
        return r * brows + brows - 1 >= c * bcols

    def piece(index):
        return pl.ds(index * cap, cap)

    def hop(to_row, to_col):
        target = to_row * ncol + to_col
        return pltpu.make_async_remote_copy(
            src_ref=blocks.at[piece(target)], dst_ref=middle.at[piece(to_row * ncol + col)],
            send_sem=send.at[target], recv_sem=middle_recv.at[to_row * ncol + col],
            device_id=(row, to_col), device_id_type=MESH,
        )

    def relay(to_row, from_col):
        return pltpu.make_async_remote_copy(
            src_ref=middle.at[piece(to_row * ncol + from_col)],
            dst_ref=arrived.at[piece(row * ncol + from_col)],
            send_sem=pass_send.at[to_row * ncol + from_col],
            recv_sem=recv.at[row * ncol + from_col],
            device_id=(to_row, col), device_id_type=MESH,
        )

    def straight(source, target):
        return pltpu.make_async_remote_copy(
            src_ref=blocks.at[piece(target)], dst_ref=arrived.at[piece(source)],
            send_sem=send.at[target], recv_sem=recv.at[source],
            device_id=(target // ncol, target % ncol), device_id_type=MESH,
        )

    def label_copy(source, target):
        return pltpu.make_async_remote_copy(
            src_ref=labels.at[target], dst_ref=marks.at[source],
            send_sem=label_send.at[target], recv_sem=label_recv.at[source],
            device_id=(target // ncol, target % ncol), device_id_type=MESH,
        )

    own_blocks = pltpu.make_async_copy(blocks.at[piece(me)], arrived.at[piece(me)], local_sem.at[0])
    own_labels = pltpu.make_async_copy(labels.at[me], marks.at[me], local_sem.at[1])

    order = [(nrow // 2 + i) % nrow for i in range(nrow)]
    order = [o for o in order if o != 0]

    @pl.when(active(row, col))
    def _():
        for o in order:
            straight(me, (row + o) % nrow * ncol + col).start()

        def step(j, carry):
            to_col = (col + j) % ncol
            for o in order:
                hop((row + o) % nrow, to_col).start()
            return carry

        lax.fori_loop(1, ncol, step, 0)

        def inside(j, carry):
            straight(me, row * ncol + (col + j) % ncol).start()
            return carry

        lax.fori_loop(1, ncol, inside, 0)

        def label_step(d, carry):
            label_copy(me, (me + d) % n).start()
            return carry

        lax.fori_loop(1, n, label_step, 0)
        own_blocks.start()
        own_labels.start()

    def landed(to_row, from_col):
        return pltpu.make_async_remote_copy(
            src_ref=blocks.at[piece(0)],
            dst_ref=middle.at[piece(to_row * ncol + from_col)],
            send_sem=send.at[0], recv_sem=middle_recv.at[to_row * ncol + from_col],
            device_id=(row, from_col), device_id_type=MESH,
        )

    def forward(j, carry):
        from_col = (col + ncol - j) % ncol
        previous = (col + ncol - j + 1) % ncol
        mine = active(row, from_col)

        for o in order:
            to_row = (row + o) % nrow

            @pl.when(mine & (to_row > row))
            def _(to_row=to_row):
                landed(to_row, from_col).wait_recv()
                relay(to_row, from_col).start()

        @pl.when((row < nrow - 1) & active(row + 1, previous))
        def _():
            straight((row + 1) * ncol + previous, 0).wait_recv()

        for o in order:
            to_row = (row + o) % nrow

            @pl.when(mine & (to_row < row))
            def _(to_row=to_row):
                landed(to_row, from_col).wait_recv()
                relay(to_row, from_col).start()

        return carry

    lax.fori_loop(1, ncol, forward, 0)

    def arrive(s, carry):
        @pl.when((s != me) & active(s // ncol, s % ncol))
        def _():
            label_copy(s, 0).wait_recv()

            @pl.when((s // ncol != row + 1) | (s % ncol == (col + 1) % ncol))
            def _():
                straight(s, 0).wait_recv()

        return carry

    lax.fori_loop(0, n, arrive, 0)

    def passed(j, carry):
        from_col = (col + ncol - j) % ncol

        @pl.when(active(row, from_col))
        def _():
            for o in order:
                relay((row + o) % nrow, from_col).wait_send()

        return carry

    lax.fori_loop(1, ncol, passed, 0)

    @pl.when(active(row, col))
    def _():
        def drain(d, carry):
            target = (me + d) % n
            label_copy(me, target).wait_send()
            straight(me, target).wait_send()
            return carry

        lax.fori_loop(1, n, drain, 0)
        own_blocks.wait()
        own_labels.wait()


def exchange(blocks, labels, brows, bcols, cap):
    nrow, ncol = lax.axis_size("row"), lax.axis_size("col")
    n = nrow * ncol
    dma = pltpu.SemaphoreType.DMA
    return pl.pallas_call(
        functools.partial(exchange_kernel, nrow, ncol, brows, bcols, cap),
        out_shape=(
            jax.ShapeDtypeStruct(blocks.shape, blocks.dtype),
            jax.ShapeDtypeStruct(labels.shape, labels.dtype),
        ),
        in_specs=[ANY, VMEM],
        out_specs=(ANY, VMEM),
        scratch_shapes=[
            pltpu.VMEM(blocks.shape, blocks.dtype),
            dma((n,)), dma((n,)), dma((n,)), dma((n,)), dma((n,)), dma((n,)), dma((2,)),
        ],
        compiler_params=pltpu.CompilerParams(has_side_effects=True),
        name="exchange",
    )(blocks, labels)


def add_kernel(ncol, brows, bcols, cap, marks, parent, arrived, out, held, sem, parent_sem):
    n = arrived.shape[0] // cap

    def each(body):
        def step(s, carry):
            @pl.when(s // ncol * brows + brows - 1 >= s % ncol * bcols)
            def _():
                body(s)

            return carry

        lax.fori_loop(0, n, step, 0)

    def fetch(s):
        part = pl.ds(s * cap, cap)
        return pltpu.make_async_copy(arrived.at[part], held.at[part], sem.at[s])

    whole = pltpu.make_async_copy(parent, out, parent_sem)
    whole.start()
    each(lambda s: fetch(s).start())
    whole.wait()

    def add(s):
        fetch(s).wait()
        for k in range(cap):
            m = marks[s * cap + k]

            @pl.when(m >= 0)
            def _(k=k, m=m):
                out[m] = out[m] + held[s * cap + k]

    each(add)


def add_blocks(marks, parent, arrived, brows, bcols, cap):
    n = arrived.shape[0] // cap
    return pl.pallas_call(
        functools.partial(add_kernel, lax.axis_size("col"), brows, bcols, cap),
        out_shape=jax.ShapeDtypeStruct(parent.shape, parent.dtype),
        in_specs=[SMEM, ANY, ANY],
        out_specs=VMEM,
        scratch_shapes=[
            pltpu.VMEM(arrived.shape, arrived.dtype),
            pltpu.SemaphoreType.DMA((n,)),
            pltpu.SemaphoreType.DMA,
        ],
        name="add_blocks",
    )(marks, parent, arrived)


def local(front, inverses, block_owner, block_slot, parent_in):
    width = inverses.shape[1]
    nrow, ncol = lax.axis_size("row"), lax.axis_size("col")
    devices = nrow * ncol
    row, col = lax.axis_index("row"), lax.axis_index("col")
    brows, bcols = block_owner.shape
    edge = parent_in.shape[1]
    count = brows * bcols
    cap = max(1, (count + devices - 1) // devices)

    owners = block_owner.reshape(1, count)
    slots = block_slot.reshape(1, 1, count)
    hit = owners == jnp.arange(devices, dtype=jnp.int32)[:, None]
    before = jnp.arange(count)[:, None] < jnp.arange(count)[None, :]
    rank = jnp.dot(
        hit.astype(jnp.float32), before.astype(jnp.float32), preferred_element_type=jnp.float32
    ).astype(jnp.int32)
    chosen = hit[:, None, :] & (rank[:, None, :] == jnp.arange(cap, dtype=jnp.int32)[:, None])
    position = jnp.arange(count, dtype=jnp.int32)
    place = jnp.arange(devices * cap, dtype=jnp.int32).reshape(devices, cap) % count
    filled = jnp.any(chosen, axis=2)
    where = jnp.where(filled, jnp.sum(jnp.where(chosen, position, 0), axis=2), place)
    where = where.reshape(devices * cap)
    label = jnp.sum(jnp.where(chosen, slots + 1, 0), axis=2) - 1
    labels = jnp.broadcast_to(
        jnp.pad(label, ((0, 0), (0, 128 - cap)), constant_values=-1)[:, None, :], (devices, 8, 128)
    )

    columns, rows, corner = spread(front, width)
    below, right = corner[0], corner[1]
    rows_one = rows[:width]
    factor_one = matmul(columns[:, :width], inverses[0])
    factor_two = matmul(columns[:, width:] - matmul(factor_one, right), inverses[1])
    rows_two = rows[width:] - matmul(matmul(below, inverses[0]), rows_one)
    updated = front - matmul(factor_one, rows_one) - matmul(factor_two, rows_two)
    piece = front.shape[0] // ncol
    panels = jnp.concatenate(
        [
            lax.dynamic_slice_in_dim(factor_one, col * piece, piece, 0),
            lax.dynamic_slice_in_dim(factor_two, col * piece, piece, 0),
        ],
        axis=1,
    )

    blocks = gather_blocks(where, updated, bcols, edge)
    arrived, marks = exchange(blocks, labels, brows, bcols, cap)
    sources = jnp.arange(devices, dtype=jnp.int32)
    sends = sources // ncol * brows + brows - 1 >= sources % ncol * bcols
    marks = jnp.where(sends[:, None], marks[:, 0, :cap], -1).reshape(devices * cap)
    parent_out = add_blocks(marks, parent_in, arrived, brows, bcols, cap)
    return (updated, panels, parent_out)


def solution(mesh):
    in_specs = (
        P("row", "col"),
        P(),
        P("row", "col"),
        P("row", "col"),
        P(("row", "col"), None, None),
    )
    out_specs = (P("row", "col"), P(("row", "col"), None), P(("row", "col"), None, None))
    return jax.shard_map(local, mesh=mesh, in_specs=in_specs, out_specs=out_specs, check_vma=False)
```

```python
import functools

import jax
import jax.numpy as jnp
from jax import lax
from jax.experimental import pallas as pl
from jax.experimental.pallas import tpu as pltpu
from jax.sharding import PartitionSpec as P

MESH = pl.DeviceIdType.MESH
ANY = pl.BlockSpec(memory_space=pl.ANY)
VMEM = pl.BlockSpec(memory_space=pltpu.VMEM)
SMEM = pl.BlockSpec(memory_space=pltpu.SMEM)


def matmul(left_side, right_side):
    return jnp.dot(
        left_side, right_side, preferred_element_type=jnp.float32, precision=lax.Precision.HIGH
    )


def chip_paths(chips):
    order = [i ^ (i >> 1) for i in range(chips)]
    if sorted(order) != list(range(chips)):
        order = list(range(chips))
    return order, [order[0]] + order[1:][::-1]


def pick(value, pairs, default):
    out = jnp.int32(default)
    for key, result in pairs:
        out = jnp.where(value == key, jnp.int32(result), out)
    return out


def spread_kernel(
    nrow, ncol, width, front, cols_out, rows_out, corner_out,
    stage_cols, stage_rows, stage_corner,
    row_send, row_recv, half_recv, chain_send, side_send, local_sem,
):
    row = lax.axis_index("row")
    col = lax.axis_index("col")
    chips = ncol // 2
    chip = col // 2
    core = col % 2
    paths = chip_paths(chips)
    steps = 32
    half = cols_out.shape[0] // 2
    ch = half // steps
    quarter = steps // 2
    rh = width // quarter
    corner = steps // 4
    kh = width // 2 // corner
    nexts = [pick(chip, list(zip(p[:-1], p[1:])), 0) for p in paths]
    next_chip = jnp.where(core == 0, nexts[0], nexts[1])
    is_last = jnp.where(core == 0, chip == paths[0][-1], chip == paths[1][-1])
    pieces = ((1, 0), (0, 1), (0, 0), (1, 1))

    def row_copy(src, q, k):
        s = (pl.ds(pieces[q][0] * width + k * rh, rh), pl.ds(pieces[q][1] * width, width))
        return pltpu.make_async_remote_copy(
            src_ref=src.at[s], dst_ref=rows_out.at[s],
            send_sem=row_send.at[q * quarter + k], recv_sem=row_recv.at[q * quarter + k],
            device_id=(row + 1, col), device_id_type=MESH,
        )

    def col_copy(src, h, k, send, target):
        s = pl.ds(h * half + k * ch, ch)
        return pltpu.make_async_remote_copy(
            src_ref=src.at[s, :], dst_ref=cols_out.at[s, :],
            send_sem=send.at[h, k], recv_sem=half_recv.at[h, k],
            device_id=(row, target), device_id_type=MESH,
        )

    def corner_copy(src, first, h, k, i, send, target):
        at = h * (width // 2) + k * kh
        to = corner_out.at[i, pl.ds(at, kh), :]
        if first:
            src = src.at[pl.ds(pieces[i][0] * width + at, kh), pl.ds(pieces[i][1] * width, width)]
        else:
            src = to
        slot = steps + i * corner + k
        return pltpu.make_async_remote_copy(
            src_ref=src, dst_ref=to,
            send_sem=send.at[h, slot], recv_sem=half_recv.at[h, slot],
            device_id=(row, target), device_id_type=MESH,
        )

    local_cols = pltpu.make_async_copy(front, stage_cols, local_sem.at[0])
    local_rows = pltpu.make_async_copy(
        front.at[pl.ds(0, 2 * width), :], stage_rows, local_sem.at[1]
    )

    def local_corner(src, i):
        return pltpu.make_async_copy(
            src.at[pl.ds(pieces[i][0] * width, width), pl.ds(pieces[i][1] * width, width)],
            stage_corner.at[i], local_sem.at[2 + i],
        )

    def store(stage, out, i):
        return pltpu.make_async_copy(stage, out, local_sem.at[4 + i])

    def source_sends(h, make):
        if chips > 1:
            make(h, chain_send, paths[h][1] * 2 + h).start()
        make(h, side_send, 1).start()

    @pl.when(row == 0)
    def _():
        if nrow > 1:
            for q in range(4):
                def first(k, carry, q=q):
                    row_copy(front, q, k).start()
                    return carry

                lax.fori_loop(0, quarter, first, 0)
        local_rows.start()

    @pl.when(col == 0)
    def _():
        def first(k, carry):
            for h in range(2):
                source_sends(h, lambda h, send, to: col_copy(front, h, k, send, to))
            return carry

        lax.fori_loop(0, steps, first, 0)
        local_cols.start()

    def pass_rows(q, k):
        if nrow > 1:
            @pl.when(row > 0)
            def _():
                row_copy(rows_out, q, k).wait_recv()

            @pl.when((row > 0) & (row < nrow - 1))
            def _():
                row_copy(rows_out, q, k).start()

    def pass_columns(make):
        @pl.when(chip > 0)
        def _():
            make(core, chain_send, 0).wait_recv()
            make(core, side_send, chip * 2 + 1 - core).start()

            @pl.when(jnp.logical_not(is_last))
            def _():
                make(core, chain_send, next_chip * 2 + core).start()

    for q in range(2):
        def both(k, carry, q=q):
            pass_rows(q, k)
            pass_columns(lambda h, send, to: col_copy(cols_out, h, q * quarter + k, send, to))
            return carry

        lax.fori_loop(0, quarter, both, 0)

    for i in range(2):
        @pl.when((col == 0) & (row == 0))
        def _(i=i):
            local_corner(front, i).start()

            def give(k, carry):
                for h in range(2):
                    source_sends(
                        h, lambda h, send, to: corner_copy(front, True, h, k, i, send, to)
                    )
                return carry

            lax.fori_loop(0, corner, give, 0)

        @pl.when((col == 0) & (row > 0))
        def _(i=i):
            local_corner(rows_out, i).start()

            def give(k, carry):
                for h in range(2):
                    source_sends(
                        h, lambda h, send, to: corner_copy(rows_out, True, h, k, i, send, to)
                    )
                return carry

            lax.fori_loop(0, corner, give, 0)

    for i in range(2):
        def third(k, carry, i=i):
            pass_rows(2, i * corner + k)
            pass_columns(
                lambda h, send, to: corner_copy(corner_out, False, h, k, i, send, to)
            )
            return carry

        lax.fori_loop(0, corner, third, 0)

    @pl.when(row == 0)
    def _():
        local_rows.wait()
        store(stage_rows, rows_out, 1).start()

    @pl.when(col == 0)
    def _():
        local_cols.wait()
        store(stage_cols, cols_out, 0).start()
        for i in range(2):
            local_corner(rows_out, i).wait()
        store(stage_corner, corner_out, 2).start()

    def fourth(k, carry):
        pass_rows(3, k)
        return carry

    lax.fori_loop(0, quarter, fourth, 0)

    if nrow > 1:
        @pl.when(row < nrow - 1)
        def _():
            for q in range(4):
                def sent(k, carry, q=q):
                    row_copy(rows_out, q, k).wait_send()
                    return carry

                lax.fori_loop(0, quarter, sent, 0)

    def drain(make):
        @pl.when(col == 0)
        def _():
            for h in range(2):
                if chips > 1:
                    make(h, chain_send).wait_send()
                make(h, side_send).wait_send()

        @pl.when(col == 1)
        def _():
            for h in range(2):
                make(h, chain_send).wait_recv()

        @pl.when(chip > 0)
        def _():
            make(1 - core, chain_send).wait_recv()
            make(core, side_send).wait_send()

            @pl.when(jnp.logical_not(is_last))
            def _():
                make(core, chain_send).wait_send()

    def drain_columns(k, carry):
        drain(lambda h, send: col_copy(cols_out, h, k, send, 0))
        return carry

    lax.fori_loop(0, steps, drain_columns, 0)
    for i in range(2):
        def drain_corner(k, carry, i=i):
            drain(lambda h, send: corner_copy(corner_out, False, h, k, i, send, 0))
            return carry

        lax.fori_loop(0, corner, drain_corner, 0)

    @pl.when(row == 0)
    def _():
        store(stage_rows, rows_out, 1).wait()

    @pl.when(col == 0)
    def _():
        store(stage_cols, cols_out, 0).wait()
        store(stage_corner, corner_out, 2).wait()


def spread(front, width):
    nrow, ncol = lax.axis_size("row"), lax.axis_size("col")
    dma = pltpu.SemaphoreType.DMA
    shape = functools.partial(jax.ShapeDtypeStruct, dtype=front.dtype)
    return pl.pallas_call(
        functools.partial(spread_kernel, nrow, ncol, width),
        out_shape=(
            shape((front.shape[0], 2 * width)),
            shape((2 * width, front.shape[1])),
            shape((2, width, width)),
        ),
        in_specs=[ANY],
        out_specs=(ANY, ANY, ANY),
        scratch_shapes=[
            pltpu.VMEM((front.shape[0], 2 * width), front.dtype),
            pltpu.VMEM((2 * width, front.shape[1]), front.dtype),
            pltpu.VMEM((2, width, width), front.dtype),
            dma((64,)), dma((64,)), dma((2, 48)), dma((2, 48)), dma((2, 48)), dma((7,)),
        ],
        compiler_params=pltpu.CompilerParams(has_side_effects=True),
        name="spread",
    )(front)


def gather_kernel(count, bcols, where, updated, out, sem):
    edge = out.shape[1]

    def step(s, carry):
        b = where[s]
        src = updated.at[
            pl.ds(pl.multiple_of(b // bcols * edge, edge), edge),
            pl.ds(pl.multiple_of(b % bcols * edge, edge), edge),
        ]
        pltpu.make_async_copy(src, out.at[s], sem).start()
        return carry

    lax.fori_loop(0, count, step, 0)
    pltpu.make_async_copy(out, out, sem).wait()


def gather_blocks(where, updated, bcols, edge):
    count = where.shape[0]
    return pl.pallas_call(
        functools.partial(gather_kernel, count, bcols),
        out_shape=jax.ShapeDtypeStruct((count, edge, edge), updated.dtype),
        in_specs=[SMEM, ANY],
        out_specs=VMEM,
        scratch_shapes=[pltpu.SemaphoreType.DMA],
        name="gather_blocks",
    )(where, updated)


def exchange_kernel(
    nrow, ncol, brows, bcols, cap, blocks, labels, arrived, marks, middle,
    send, middle_recv, pass_send, recv, label_send, label_recv, local_sem,
):
    row = lax.axis_index("row")
    col = lax.axis_index("col")
    n = nrow * ncol
    me = row * ncol + col

    def active(r, c):
        return r * brows + brows - 1 >= c * bcols

    def piece(index):
        return pl.ds(index * cap, cap)

    def hop(to_row, to_col):
        target = to_row * ncol + to_col
        return pltpu.make_async_remote_copy(
            src_ref=blocks.at[piece(target)], dst_ref=middle.at[piece(to_row * ncol + col)],
            send_sem=send.at[target], recv_sem=middle_recv.at[to_row * ncol + col],
            device_id=(row, to_col), device_id_type=MESH,
        )

    def relay(to_row, from_col):
        return pltpu.make_async_remote_copy(
            src_ref=middle.at[piece(to_row * ncol + from_col)],
            dst_ref=arrived.at[piece(row * ncol + from_col)],
            send_sem=pass_send.at[to_row * ncol + from_col],
            recv_sem=recv.at[row * ncol + from_col],
            device_id=(to_row, col), device_id_type=MESH,
        )

    def straight(source, target):
        return pltpu.make_async_remote_copy(
            src_ref=blocks.at[piece(target)], dst_ref=arrived.at[piece(source)],
            send_sem=send.at[target], recv_sem=recv.at[source],
            device_id=(target // ncol, target % ncol), device_id_type=MESH,
        )

    def label_copy(source, target):
        return pltpu.make_async_remote_copy(
            src_ref=labels.at[target], dst_ref=marks.at[source],
            send_sem=label_send.at[target], recv_sem=label_recv.at[source],
            device_id=(target // ncol, target % ncol), device_id_type=MESH,
        )

    own_blocks = pltpu.make_async_copy(blocks.at[piece(me)], arrived.at[piece(me)], local_sem.at[0])
    own_labels = pltpu.make_async_copy(labels.at[me], marks.at[me], local_sem.at[1])

    order = [(nrow // 2 + i) % nrow for i in range(nrow)]
    order = [o for o in order if o != 0]

    @pl.when(active(row, col))
    def _():
        for o in order:
            straight(me, (row + o) % nrow * ncol + col).start()

        def step(j, carry):
            to_col = (col + j) % ncol
            for o in order:
                hop((row + o) % nrow, to_col).start()
            return carry

        lax.fori_loop(1, ncol, step, 0)

        def inside(j, carry):
            straight(me, row * ncol + (col + j) % ncol).start()
            return carry

        lax.fori_loop(1, ncol, inside, 0)

        def label_step(d, carry):
            label_copy(me, (me + d) % n).start()
            return carry

        lax.fori_loop(1, n, label_step, 0)
        own_blocks.start()
        own_labels.start()

    def landed(to_row, from_col):
        return pltpu.make_async_remote_copy(
            src_ref=blocks.at[piece(0)],
            dst_ref=middle.at[piece(to_row * ncol + from_col)],
            send_sem=send.at[0], recv_sem=middle_recv.at[to_row * ncol + from_col],
            device_id=(row, from_col), device_id_type=MESH,
        )

    def forward(j, carry):
        from_col = (col + ncol - j) % ncol
        mine = active(row, from_col)

        for o in order:
            to_row = (row + o) % nrow

            @pl.when(mine & (to_row > row))
            def _(to_row=to_row):
                landed(to_row, from_col).wait_recv()
                relay(to_row, from_col).start()

        for o in order:
            to_row = (row + o) % nrow

            @pl.when(mine & (to_row < row))
            def _(to_row=to_row):
                landed(to_row, from_col).wait_recv()
                relay(to_row, from_col).start()

        return carry

    lax.fori_loop(1, ncol, forward, 0)

    def arrive(s, carry):
        @pl.when((s != me) & active(s // ncol, s % ncol))
        def _():
            label_copy(s, 0).wait_recv()
            straight(s, 0).wait_recv()

        return carry

    lax.fori_loop(0, n, arrive, 0)

    def passed(j, carry):
        from_col = (col + ncol - j) % ncol

        @pl.when(active(row, from_col))
        def _():
            for o in order:
                relay((row + o) % nrow, from_col).wait_send()

        return carry

    lax.fori_loop(1, ncol, passed, 0)

    @pl.when(active(row, col))
    def _():
        def drain(d, carry):
            target = (me + d) % n
            label_copy(me, target).wait_send()
            straight(me, target).wait_send()
            return carry

        lax.fori_loop(1, n, drain, 0)
        own_blocks.wait()
        own_labels.wait()


def exchange(blocks, labels, brows, bcols, cap):
    nrow, ncol = lax.axis_size("row"), lax.axis_size("col")
    n = nrow * ncol
    dma = pltpu.SemaphoreType.DMA
    return pl.pallas_call(
        functools.partial(exchange_kernel, nrow, ncol, brows, bcols, cap),
        out_shape=(
            jax.ShapeDtypeStruct(blocks.shape, blocks.dtype),
            jax.ShapeDtypeStruct(labels.shape, labels.dtype),
        ),
        in_specs=[ANY, VMEM],
        out_specs=(ANY, VMEM),
        scratch_shapes=[
            pltpu.VMEM(blocks.shape, blocks.dtype),
            dma((n,)), dma((n,)), dma((n,)), dma((n,)), dma((n,)), dma((n,)), dma((2,)),
        ],
        compiler_params=pltpu.CompilerParams(has_side_effects=True),
        name="exchange",
    )(blocks, labels)


def add_kernel(ncol, brows, bcols, cap, marks, parent, arrived, out, held, sem, parent_sem):
    n = arrived.shape[0] // cap

    def each(body):
        def step(s, carry):
            @pl.when(s // ncol * brows + brows - 1 >= s % ncol * bcols)
            def _():
                body(s)

            return carry

        lax.fori_loop(0, n, step, 0)

    def fetch(s):
        part = pl.ds(s * cap, cap)
        return pltpu.make_async_copy(arrived.at[part], held.at[part], sem.at[s])

    whole = pltpu.make_async_copy(parent, out, parent_sem)
    whole.start()
    each(lambda s: fetch(s).start())
    whole.wait()

    def add(s):
        fetch(s).wait()
        for k in range(cap):
            m = marks[s * cap + k]

            @pl.when(m >= 0)
            def _(k=k, m=m):
                out[m] = out[m] + held[s * cap + k]

    each(add)


def add_blocks(marks, parent, arrived, brows, bcols, cap):
    n = arrived.shape[0] // cap
    return pl.pallas_call(
        functools.partial(add_kernel, lax.axis_size("col"), brows, bcols, cap),
        out_shape=jax.ShapeDtypeStruct(parent.shape, parent.dtype),
        in_specs=[SMEM, ANY, ANY],
        out_specs=VMEM,
        scratch_shapes=[
            pltpu.VMEM(arrived.shape, arrived.dtype),
            pltpu.SemaphoreType.DMA((n,)),
            pltpu.SemaphoreType.DMA,
        ],
        name="add_blocks",
    )(marks, parent, arrived)


def local(front, inverses, block_owner, block_slot, parent_in):
    width = inverses.shape[1]
    nrow, ncol = lax.axis_size("row"), lax.axis_size("col")
    devices = nrow * ncol
    row, col = lax.axis_index("row"), lax.axis_index("col")
    brows, bcols = block_owner.shape
    edge = parent_in.shape[1]
    count = brows * bcols
    cap = max(1, (count + devices - 1) // devices)

    owners = block_owner.reshape(1, count)
    slots = block_slot.reshape(1, 1, count)
    hit = owners == jnp.arange(devices, dtype=jnp.int32)[:, None]
    before = jnp.arange(count)[:, None] < jnp.arange(count)[None, :]
    rank = jnp.dot(
        hit.astype(jnp.float32), before.astype(jnp.float32), preferred_element_type=jnp.float32
    ).astype(jnp.int32)
    chosen = hit[:, None, :] & (rank[:, None, :] == jnp.arange(cap, dtype=jnp.int32)[:, None])
    position = jnp.arange(count, dtype=jnp.int32)
    place = jnp.arange(devices * cap, dtype=jnp.int32).reshape(devices, cap) % count
    filled = jnp.any(chosen, axis=2)
    where = jnp.where(filled, jnp.sum(jnp.where(chosen, position, 0), axis=2), place)
    where = where.reshape(devices * cap)
    label = jnp.sum(jnp.where(chosen, slots + 1, 0), axis=2) - 1
    labels = jnp.broadcast_to(
        jnp.pad(label, ((0, 0), (0, 128 - cap)), constant_values=-1)[:, None, :], (devices, 8, 128)
    )

    columns, rows, corner = spread(front, width)
    below, right = corner[0], corner[1]
    rows_one = rows[:width]
    factor_one = matmul(columns[:, :width], inverses[0])
    factor_two = matmul(columns[:, width:] - matmul(factor_one, right), inverses[1])
    rows_two = rows[width:] - matmul(matmul(below, inverses[0]), rows_one)
    updated = front - matmul(factor_one, rows_one) - matmul(factor_two, rows_two)
    piece = front.shape[0] // ncol
    panels = jnp.concatenate(
        [
            lax.dynamic_slice_in_dim(factor_one, col * piece, piece, 0),
            lax.dynamic_slice_in_dim(factor_two, col * piece, piece, 0),
        ],
        axis=1,
    )

    blocks = gather_blocks(where, updated, bcols, edge)
    arrived, marks = exchange(blocks, labels, brows, bcols, cap)
    sources = jnp.arange(devices, dtype=jnp.int32)
    sends = sources // ncol * brows + brows - 1 >= sources % ncol * bcols
    marks = jnp.where(sends[:, None], marks[:, 0, :cap], -1).reshape(devices * cap)
    parent_out = add_blocks(marks, parent_in, arrived, brows, bcols, cap)
    return (updated, panels, parent_out)


def solution(mesh):
    in_specs = (
        P("row", "col"),
        P(),
        P("row", "col"),
        P("row", "col"),
        P(("row", "col"), None, None),
    )
    out_specs = (P("row", "col"), P(("row", "col"), None), P(("row", "col"), None, None))
    return jax.shard_map(local, mesh=mesh, in_specs=in_specs, out_specs=out_specs, check_vma=False)
```
